32 devices in a mesh: req: 2 (over y), ctx: 8 (over z, x), tp: 2 (over core).
Axes of the slice: x: 2, y: 2, z: 4, core: 2. Of those that a mesh axis runs over, the one named last changes fastest.
Arguments:
- queries: bfloat16 [32, 5120], P(('req', 'ctx'), 'tp'), parts along dimension 0, may hold values from -9 to 9, as said below
- repeat_block_keys: bfloat16 [32, 1024], P(('req', 'ctx'), 'tp'), parts along dimension 0, may hold values from -12 to 12
- context_keys: bfloat16 [16384, 1024], P(('req', 'ctx'), 'tp'), parts along dimension 0, may hold values from -15 to 15, as said below
Outputs:
- importance: float32 [8, 16384], P('tp', ('req', 'ctx')), parts along dimension 1
The draws below stay inside these ranges and needn't reach their ends.
There are 2 independent parts, one for each index of `req`. The reference program is written for one: setup_inputs(seed, part) draws one part's arguments, and reference() takes and returns one part's arrays. A program takes and returns all parts, laid end to end along the dimension named above; each array names one. Nothing has to cross between parts.
Inputs may be any that keep to these rules, and one draw needn't show every extreme that they name: queries of order one. `context_keys`: cached keys of order one.
All inputs are finite; a program needn't handle non-finite values.
Results may differ from the reference program's by a relative error of at most 0.0003.
Values may be sent and summed in bfloat16 or wider, within the bound.
A program may use at most 64 MiB of HBM per device.

```python
import math
import jax
import jax.numpy as jnp
from jax import lax

HQ = 40
KEY_HEADS = 8
HEAD_SIZE = 128
HEADS_PER_KEY = 5
CONTEXT_TOKENS = 8192
REPEAT_TOKENS = 16


def draw_context_keys(key, part):
    position = jnp.arange(CONTEXT_TOKENS, dtype=jnp.float32)
    ramp_factor = 0.8 + 0.8 * position / CONTEXT_TOKENS
    base_sample = jnp.clip(jax.random.normal(jax.random.fold_in(key, 11), (CONTEXT_TOKENS, KEY_HEADS * HEAD_SIZE), jnp.float32), -5.0, 5.0)
    spread = jnp.exp(jax.random.uniform(jax.random.fold_in(key, 12), (CONTEXT_TOKENS, 1), jnp.float32, -0.6, 0.6))
    key_rows = base_sample * spread * ramp_factor[:, None]
    return key_rows.astype(jnp.bfloat16)


def draw_queries(key, part):
    base_sample = jnp.clip(jax.random.normal(jax.random.fold_in(key, 21), (REPEAT_TOKENS, HQ * HEAD_SIZE), jnp.float32), -4.0, 4.0)
    return base_sample.astype(jnp.bfloat16)


def block_scale(stream_key, shape, cuts, smallest, high):
    def one(dim, blocks):
        heights = jax.random.uniform(jax.random.fold_in(jax.random.fold_in(stream_key, 6), dim), (blocks,), jnp.float32, smallest / len(cuts), high / len(cuts))
        return jnp.repeat(jnp.exp(heights), shape[dim] // blocks).reshape((-1,) + (1,) * (len(shape) - dim - 1))

    level = one(*cuts[0])
    for cut in cuts[1:]:
        level = level * one(*cut)
    return level


def gaussian(rng, extent, scale, limit, cuts=(), held_as=jnp.bfloat16):
    drawn = jax.random.normal(rng, extent, jnp.float32) * scale
    if len(cuts) > 0:
        drawn = block_scale(rng, extent, cuts, -0.22, 0.18) * drawn
    return jnp.clip(drawn, min=-limit, max=limit).astype(held_as)


def setup_inputs(seed: int = 0, part: int = 0) -> dict:
    key_list = jax.random.split(jax.random.key(seed), 4)
    part_splits = jax.random.split(jax.random.fold_in(key_list[3], part), 4)
    queries = draw_queries(jax.random.fold_in(jax.random.fold_in(key_list[3], part), 71), part)
    repeat_block_keys = gaussian(part_splits[1], (REPEAT_TOKENS, KEY_HEADS * HEAD_SIZE), 3.0, 12.0, ((0, 8), (1, 2)))
    context_keys = draw_context_keys(jax.random.fold_in(jax.random.fold_in(key_list[3], part), 71), part)
    return {"queries": queries, "repeat_block_keys": repeat_block_keys, "context_keys": context_keys}


NEG_FILL = -1e+30

def head_scores(query_rows, key_rows):
    score_scale = 1.0 / math.sqrt(HEAD_SIZE)
    return jnp.einsum('rgud,ngd->rgun', query_rows, key_rows, precision=lax.Precision.HIGHEST) * score_scale

def reference(queries, repeat_block_keys, context_keys):
    query_single_float = queries.astype(jnp.float32).reshape(REPEAT_TOKENS, KEY_HEADS, HEADS_PER_KEY, HEAD_SIZE)
    repeat_single_float = repeat_block_keys.astype(jnp.float32).reshape(REPEAT_TOKENS, KEY_HEADS, HEAD_SIZE)
    row_index = jnp.arange(REPEAT_TOKENS, dtype=jnp.int32)
    causal = row_index[None, :] <= row_index[:, None]
    self_scores = jnp.where(causal[:, None, None, :], head_scores(query_single_float, repeat_single_float), NEG_FILL)
    start_max = lax.optimization_barrier(jnp.max(self_scores, axis=-1))
    start_sum = lax.optimization_barrier(jnp.sum(jnp.exp(self_scores - start_max[..., None]), axis=-1))
    block_length = math.gcd(CONTEXT_TOKENS, 2048)
    block_total = context_keys.reshape(CONTEXT_TOKENS // block_length, block_length, KEY_HEADS, HEAD_SIZE)

    def fold_block(carry, block_keys):
        run_max, run_sum = carry
        scores = head_scores(query_single_float, block_keys.astype(jnp.float32))
        new_max = jnp.maximum(run_max, lax.optimization_barrier(jnp.max(scores, axis=-1)))
        run_sum = run_sum * jnp.exp(run_max - new_max) + lax.optimization_barrier(jnp.sum(jnp.exp(scores - new_max[..., None]), axis=-1))
        return ((new_max, run_sum), None)
    (row_max, row_total), unused = lax.scan(fold_block, (start_max, start_sum), block_total)
    log_shift = row_max + jnp.log(row_total)

    def block_importance(block_keys):
        scores = head_scores(query_single_float, block_keys.astype(jnp.float32))
        return lax.optimization_barrier(jnp.max(scores - log_shift[..., None], axis=(0, 2)))
    tokens_per_block = lax.map(block_importance, block_total)
    return jnp.transpose(tokens_per_block, (1, 0, 2)).reshape(KEY_HEADS, CONTEXT_TOKENS)
```

```python
import functools
import math

import jax
import jax.numpy as jnp
from jax import lax
from jax.experimental import pallas as pl
from jax.experimental.pallas import tpu as pltpu
from jax.sharding import PartitionSpec as P

HEAD_SIZE = 128
LANES = 128
BLOCK_ROWS = 16
NEG_FILL = -1e30
SCALE = 1.0 / math.sqrt(HEAD_SIZE)
EXP2_SCALE = SCALE * math.log2(math.e)
NT = (((1,), (1,)), ((), ()))


def kernel(
    n, group, q_ref, own_ref, k_ref, out_ref,
    q_all, own, keys, q_block, scores, lse,
    q_send, q_recv, l_send, l_recv, local_sem,
):
    me = lax.axis_index("ctx")
    per = q_ref.shape[0]
    kv_heads = k_ref.shape[1] // HEAD_SIZE
    peers_per_block = BLOCK_ROWS // per
    blocks = n // peers_per_block
    used = group * BLOCK_ROWS
    peer = lambda offset: lax.rem(me + offset, n)

    load_keys = pltpu.make_async_copy(k_ref, keys, local_sem.at[0])
    load_own = pltpu.make_async_copy(own_ref, own, local_sem.at[1])
    load_q = pltpu.make_async_copy(q_ref, q_all.at[me], local_sem.at[2])

    barrier = pltpu.get_barrier_semaphore()
    for offset in range(1, n):
        pl.semaphore_signal(
            barrier, inc=1, device_id={"ctx": peer(offset)}, device_id_type=pl.DeviceIdType.MESH
        )
    load_keys.start()
    load_own.start()
    load_q.start()
    pl.semaphore_wait(barrier, n - 1)

    def send_q(offset, slot):
        return pltpu.make_async_remote_copy(
            src_ref=q_ref,
            dst_ref=q_all.at[slot],
            send_sem=q_send.at[offset - 1],
            recv_sem=q_recv.at[offset - 1],
            device_id={"ctx": peer(offset)},
            device_id_type=pl.DeviceIdType.MESH,
        )

    def send_lse(offset, slot):
        return pltpu.make_async_remote_copy(
            src_ref=lse.at[slot],
            dst_ref=lse.at[slot],
            send_sem=l_send.at[offset - 1],
            recv_sem=l_recv.at[offset - 1],
            device_id={"ctx": peer(offset)},
            device_id_type=pl.DeviceIdType.MESH,
        )

    for offset in range(1, n):
        send_q(offset, me).start()
    load_own.wait()
    load_keys.wait()
    load_q.wait()
    for offset in range(1, n):
        send_q(offset, peer(n - offset)).wait_recv()

    def each_block(body):
        if blocks == 1:
            body(0)
        else:
            lax.fori_loop(0, blocks, lambda b, c: (body(b), c)[1], 0)

    def queries_of(head):
        return jnp.concatenate(
            [
                q_block[:, (head * group + u) * HEAD_SIZE : (head * group + u + 1) * HEAD_SIZE]
                for u in range(group)
            ],
            axis=0,
        ).astype(jnp.bfloat16)

    def gather_block(b):
        for p in range(peers_per_block):
            q_block[p * per : (p + 1) * per, :] = q_all[b * peers_per_block + p].astype(jnp.float32)

    def stats(b):
        gather_block(b)
        lane = lax.broadcasted_iota(jnp.int32, (per, LANES), 1)
        row = b * BLOCK_ROWS + lax.rem(lane, BLOCK_ROWS)
        column = me * per + lax.broadcasted_iota(jnp.int32, (per, LANES), 0)
        causal = column <= row
        pad = jnp.zeros((LANES - used, HEAD_SIZE), jnp.bfloat16)
        for head in range(kv_heads):
            at = slice(head * HEAD_SIZE, (head + 1) * HEAD_SIZE)
            q = jnp.concatenate([queries_of(head), pad], axis=0)
            s = lax.dot_general(keys[:, at], q, NT, preferred_element_type=jnp.float32)
            t = lax.dot_general(own[:, at], q, NT, preferred_element_type=jnp.float32)
            t = jnp.where(causal, t, NEG_FILL)
            top = jnp.maximum(
                jnp.max(s, axis=0, keepdims=True), jnp.max(t, axis=0, keepdims=True)
            )
            total = jnp.sum(jnp.exp2((s - top) * EXP2_SCALE), axis=0, keepdims=True)
            total += jnp.sum(jnp.exp2((t - top) * EXP2_SCALE), axis=0, keepdims=True)
            lse[me, b, head : head + 1, :] = top * SCALE + jnp.log(total)

    lse[me] = jnp.zeros(lse.shape[1:], jnp.float32)
    each_block(stats)
    for offset in range(1, n):
        send_lse(offset, me).start()

    def keep_scores(b):
        if blocks > 1:
            gather_block(b)
        for head in range(kv_heads):
            at = slice(head * HEAD_SIZE, (head + 1) * HEAD_SIZE)
            scores[b, head] = lax.dot_general(
                queries_of(head), keys[:, at], NT, preferred_element_type=jnp.float32
            )

    each_block(keep_scores)
    for offset in range(1, n):
        send_lse(offset, peer(n - offset)).wait_recv()

    out_ref[...] = jnp.full(out_ref.shape, -jnp.inf, jnp.float32)

    def finish(b):
        parts = lse[:, b]
        top = jnp.max(parts, axis=0)
        shift = top + jnp.log(jnp.sum(jnp.exp(parts - top[None]), axis=0))
        columns = jnp.transpose(shift)
        for head in range(kv_heads):
            best = jnp.max(
                scores[b, head] * SCALE - columns[:used, head : head + 1], axis=0, keepdims=True
            )
            out_ref[head : head + 1, :] = jnp.maximum(out_ref[head : head + 1, :], best)

    each_block(finish)
    for offset in range(1, n):
        send_q(offset, me).wait_send()
        send_lse(offset, me).wait_send()


def solution(mesh):
    n = mesh.shape["ctx"]

    def on_device(queries, repeat_block_keys, context_keys):
        per, width = queries.shape
        cache_len, key_width = context_keys.shape
        kv_heads = key_width // HEAD_SIZE
        group = width // key_width
        blocks = n * per // BLOCK_ROWS
        assert blocks * BLOCK_ROWS == n * per
        return pl.pallas_call(
            functools.partial(kernel, n, group),
            out_shape=jax.ShapeDtypeStruct((kv_heads, cache_len), jnp.float32),
            in_specs=[pl.BlockSpec(memory_space=pl.ANY)] * 3,
            out_specs=pl.BlockSpec(memory_space=pltpu.VMEM),
            scratch_shapes=[
                pltpu.VMEM((n, per, width), jnp.bfloat16),
                pltpu.VMEM((per, key_width), jnp.bfloat16),
                pltpu.VMEM((cache_len, key_width), jnp.bfloat16),
                pltpu.VMEM((BLOCK_ROWS, width), jnp.float32),
                pltpu.VMEM((blocks, kv_heads, group * BLOCK_ROWS, cache_len), jnp.float32),
                pltpu.VMEM((n, blocks, 8, LANES), jnp.float32),
                pltpu.SemaphoreType.DMA((n - 1,)),
                pltpu.SemaphoreType.DMA((n - 1,)),
                pltpu.SemaphoreType.DMA((n - 1,)),
                pltpu.SemaphoreType.DMA((n - 1,)),
                pltpu.SemaphoreType.DMA((3,)),
            ],
            compiler_params=pltpu.CompilerParams(collective_id=0, has_side_effects=True),
        )(queries, repeat_block_keys, context_keys)

    placed = (P(("req", "ctx"), "tp"), P(("req", "ctx"), "tp"), P(("req", "ctx"), "tp"))
    return jax.shard_map(
        on_device, mesh=mesh, in_specs=placed, out_specs=P("tp", ("req", "ctx")), check_vma=False
    )
```

```python
import functools
import math

import jax
import jax.numpy as jnp
from jax import lax
from jax.experimental import pallas as pl
from jax.experimental.pallas import tpu as pltpu
from jax.sharding import PartitionSpec as P

HEAD_SIZE = 128
LANES = 128
BLOCK_ROWS = 16
NEG_FILL = -1e30
RESIDENT_BYTES = 2 << 20
RESIDENT_LIMIT = 8 << 20
SCALE = 1.0 / math.sqrt(HEAD_SIZE)
EXP2_SCALE = SCALE * math.log2(math.e)
NT = (((1,), (1,)), ((), ()))


def kernel(
    n, group, q_ref, own_ref, k_ref, scores, lse,
    q_all, own, keys, q_block,
    q_send, q_recv, l_send, l_recv, local_sem,
):
    me = lax.axis_index("ctx")
    per = q_ref.shape[0]
    kv_heads = k_ref.shape[1] // HEAD_SIZE
    peers_per_block = BLOCK_ROWS // per
    blocks = n // peers_per_block
    used = group * BLOCK_ROWS
    turn = 1 - 2 * (me // (n // 2))
    peer = lambda offset: lax.rem(me + turn * offset + n, n)

    load_keys = pltpu.make_async_copy(k_ref, keys, local_sem.at[0])
    load_own = pltpu.make_async_copy(own_ref, own, local_sem.at[1])
    load_q = pltpu.make_async_copy(q_ref, q_all.at[me], local_sem.at[2])

    barrier = pltpu.get_barrier_semaphore()
    for offset in reversed(range(1, n)):
        pl.semaphore_signal(
            barrier, inc=1, device_id={"ctx": peer(offset)}, device_id_type=pl.DeviceIdType.MESH
        )
    load_keys.start()
    load_own.start()
    load_q.start()
    pl.semaphore_wait(barrier, n - 1)

    def send_q(offset, slot):
        return pltpu.make_async_remote_copy(
            src_ref=q_ref,
            dst_ref=q_all.at[slot],
            send_sem=q_send.at[offset - 1],
            recv_sem=q_recv.at[slot],
            device_id={"ctx": peer(offset)},
            device_id_type=pl.DeviceIdType.MESH,
        )

    def send_lse(offset, slot):
        return pltpu.make_async_remote_copy(
            src_ref=lse.at[slot],
            dst_ref=lse.at[slot],
            send_sem=l_send.at[offset - 1],
            recv_sem=l_recv.at[slot],
            device_id={"ctx": peer(offset)},
            device_id_type=pl.DeviceIdType.MESH,
        )

    for offset in reversed(range(1, n)):
        send_q(offset, me).start()
    load_own.wait()
    load_keys.wait()
    load_q.wait()
    for offset in range(1, n):
        send_q(offset, peer(offset)).wait_recv()

    def each_block(body):
        if blocks == 1:
            body(0)
        else:
            lax.fori_loop(0, blocks, lambda b, c: (body(b), c)[1], 0)

    def queries_of(head):
        return jnp.concatenate(
            [
                q_block[:, (head * group + u) * HEAD_SIZE : (head * group + u + 1) * HEAD_SIZE]
                for u in range(group)
            ],
            axis=0,
        ).astype(jnp.bfloat16)

    def gather_block(b):
        for p in range(peers_per_block):
            q_block[p * per : (p + 1) * per, :] = q_all[b * peers_per_block + p].astype(jnp.float32)

    def stats(b):
        gather_block(b)
        lane = lax.broadcasted_iota(jnp.int32, (per, LANES), 1)
        row = b * BLOCK_ROWS + lax.rem(lane, BLOCK_ROWS)
        column = me * per + lax.broadcasted_iota(jnp.int32, (per, LANES), 0)
        causal = column <= row
        pad = jnp.zeros((LANES - used, HEAD_SIZE), jnp.bfloat16)
        for head in range(kv_heads):
            at = slice(head * HEAD_SIZE, (head + 1) * HEAD_SIZE)
            q = jnp.concatenate([queries_of(head), pad], axis=0)
            s = lax.dot_general(keys[:, at], q, NT, preferred_element_type=jnp.float32)
            t = lax.dot_general(own[:, at], q, NT, preferred_element_type=jnp.float32)
            t = jnp.where(causal, t, NEG_FILL)
            top = jnp.maximum(
                jnp.max(s, axis=0, keepdims=True), jnp.max(t, axis=0, keepdims=True)
            )
            total = jnp.sum(jnp.exp2((s - top) * EXP2_SCALE), axis=0, keepdims=True)
            total += jnp.sum(jnp.exp2((t - top) * EXP2_SCALE), axis=0, keepdims=True)
            lse[me, b, head : head + 1, :] = top * SCALE + jnp.log(total)

    lse[me] = jnp.zeros(lse.shape[1:], jnp.float32)
    each_block(stats)
    for offset in reversed(range(1, n)):
        send_lse(offset, me).start()

    def keep_scores(b):
        if blocks > 1:
            gather_block(b)
        for head in range(kv_heads):
            at = slice(head * HEAD_SIZE, (head + 1) * HEAD_SIZE)
            scores[b, head] = lax.dot_general(
                queries_of(head), keys[:, at], NT, preferred_element_type=jnp.float32
            )

    each_block(keep_scores)
    for offset in range(1, n):
        send_lse(offset, peer(offset)).wait_recv()

    for offset in range(1, n):
        send_q(offset, me).wait_send()
        send_lse(offset, me).wait_send()


def finish_kernel(scores, lse, out_ref):
    blocks, kv_heads, used, _ = scores.shape
    out_ref[...] = jnp.full(out_ref.shape, -jnp.inf, jnp.float32)

    def finish(b):
        parts = lse[:, b]
        top = jnp.max(parts, axis=0)
        shift = top + jnp.log(jnp.sum(jnp.exp(parts - top[None]), axis=0))
        columns = jnp.transpose(shift)
        for head in range(kv_heads):
            best = jnp.max(
                scores[b, head] * SCALE - columns[:used, head : head + 1], axis=0, keepdims=True
            )
            out_ref[head : head + 1, :] = jnp.maximum(out_ref[head : head + 1, :], best)

    if blocks == 1:
        finish(0)
    else:
        lax.fori_loop(0, blocks, lambda b, c: (finish(b), c)[1], 0)


def solution(mesh):
    n = mesh.shape["ctx"]

    def on_device(queries, repeat_block_keys, context_keys):
        per, width = queries.shape
        cache_len, key_width = context_keys.shape
        kv_heads = key_width // HEAD_SIZE
        group = width // key_width
        blocks = n * per // BLOCK_ROWS
        assert blocks * BLOCK_ROWS == n * per
        held_bytes = 4 * blocks * kv_heads * group * BLOCK_ROWS * cache_len
        resident = held_bytes <= RESIDENT_BYTES
        held = pltpu.VMEM if resident else jax.ShapeDtypeStruct
        finish_limit = RESIDENT_LIMIT if resident else None
        scores, lse = pl.pallas_call(
            functools.partial(kernel, n, group),
            out_shape=[
                held((blocks, kv_heads, group * BLOCK_ROWS, cache_len), jnp.float32),
                held((n, blocks, 8, LANES), jnp.float32),
            ],
            in_specs=[pl.BlockSpec(memory_space=pl.ANY)] * 3,
            out_specs=[pl.BlockSpec(memory_space=pltpu.VMEM)] * 2,
            scratch_shapes=[
                pltpu.VMEM((n, per, width), jnp.bfloat16),
                pltpu.VMEM((per, key_width), jnp.bfloat16),
                pltpu.VMEM((cache_len, key_width), jnp.bfloat16),
                pltpu.VMEM((BLOCK_ROWS, width), jnp.float32),
                pltpu.SemaphoreType.DMA((n,)),
                pltpu.SemaphoreType.DMA((n,)),
                pltpu.SemaphoreType.DMA((n,)),
                pltpu.SemaphoreType.DMA((n,)),
                pltpu.SemaphoreType.DMA((3,)),
            ],
            compiler_params=pltpu.CompilerParams(collective_id=0, has_side_effects=True),
        )(queries, repeat_block_keys, context_keys)
        return pl.pallas_call(
            finish_kernel,
            out_shape=jax.ShapeDtypeStruct((kv_heads, cache_len), jnp.float32),
            in_specs=[pl.BlockSpec(memory_space=pltpu.VMEM)] * 2,
            out_specs=pl.BlockSpec(memory_space=pltpu.VMEM),
            compiler_params=pltpu.CompilerParams(vmem_limit_bytes=finish_limit),
        )(scores, lse)

    placed = (P(("req", "ctx"), "tp"), P(("req", "ctx"), "tp"), P(("req", "ctx"), "tp"))
    return jax.shard_map(
        on_device, mesh=mesh, in_specs=placed, out_specs=P("tp", ("req", "ctx")), check_vma=False
    )
```

```python
import functools
import math

import jax
import jax.numpy as jnp
from jax import lax
from jax.experimental import pallas as pl
from jax.experimental.pallas import tpu as pltpu
from jax.sharding import PartitionSpec as P

HEAD_SIZE = 128
LANES = 128
BLOCK_ROWS = 16
NEG_FILL = -1e30
RESIDENT_BYTES = 2 << 20
RESIDENT_LIMIT = 8 << 20
SCALE = 1.0 / math.sqrt(HEAD_SIZE)
EXP2_SCALE = SCALE * math.log2(math.e)
NT = (((1,), (1,)), ((), ()))


def kernel(
    n, group, q_ref, own_ref, k_ref, scores, lse,
    q_all, own, keys, q_block,
    q_send, q_recv, l_send, l_recv, local_sem,
):
    me = lax.axis_index("ctx")
    per = q_ref.shape[0]
    kv_heads = k_ref.shape[1] // HEAD_SIZE
    peers_per_block = BLOCK_ROWS // per
    blocks = n // peers_per_block
    used = group * BLOCK_ROWS
    turn = 1 - 2 * (me // (n // 2))
    peer = lambda offset: lax.rem(me + turn * offset + n, n)

    load_keys = pltpu.make_async_copy(k_ref, keys, local_sem.at[0])
    load_own = pltpu.make_async_copy(own_ref, own, local_sem.at[1])
    load_q = pltpu.make_async_copy(q_ref, q_all.at[me], local_sem.at[2])

    barrier = pltpu.get_barrier_semaphore()
    for offset in reversed(range(1, n)):
        pl.semaphore_signal(
            barrier, inc=1, device_id={"ctx": peer(offset)}, device_id_type=pl.DeviceIdType.MESH
        )
    load_q.start()
    load_own.start()
    load_keys.start()
    load_q.wait()
    pl.semaphore_wait(barrier, n - 1)

    def send_q(offset, slot):
        return pltpu.make_async_remote_copy(
            src_ref=q_all.at[me],
            dst_ref=q_all.at[slot],
            send_sem=q_send.at[offset - 1],
            recv_sem=q_recv.at[slot],
            device_id={"ctx": peer(offset)},
            device_id_type=pl.DeviceIdType.MESH,
        )

    def send_lse(offset, slot):
        return pltpu.make_async_remote_copy(
            src_ref=lse.at[slot],
            dst_ref=lse.at[slot],
            send_sem=l_send.at[offset - 1],
            recv_sem=l_recv.at[slot],
            device_id={"ctx": peer(offset)},
            device_id_type=pl.DeviceIdType.MESH,
        )

    for offset in reversed(range(1, n)):
        send_q(offset, me).start()
    load_own.wait()
    load_keys.wait()
    for offset in range(1, n):
        send_q(offset, peer(offset)).wait_recv()

    def each_block(body):
        if blocks == 1:
            body(0)
        else:
            lax.fori_loop(0, blocks, lambda b, c: (body(b), c)[1], 0)

    def queries_of(head):
        return jnp.concatenate(
            [
                q_block[:, (head * group + u) * HEAD_SIZE : (head * group + u + 1) * HEAD_SIZE]
                for u in range(group)
            ],
            axis=0,
        ).astype(jnp.bfloat16)

    def gather_block(b):
        for p in range(peers_per_block):
            q_block[p * per : (p + 1) * per, :] = q_all[b * peers_per_block + p].astype(jnp.float32)

    def stats(b):
        gather_block(b)
        lane = lax.broadcasted_iota(jnp.int32, (per, LANES), 1)
        row = b * BLOCK_ROWS + lax.rem(lane, BLOCK_ROWS)
        column = me * per + lax.broadcasted_iota(jnp.int32, (per, LANES), 0)
        causal = column <= row
        pad = jnp.zeros((LANES - used, HEAD_SIZE), jnp.bfloat16)
        for head in range(kv_heads):
            at = slice(head * HEAD_SIZE, (head + 1) * HEAD_SIZE)
            q = jnp.concatenate([queries_of(head), pad], axis=0)
            s = lax.dot_general(keys[:, at], q, NT, preferred_element_type=jnp.float32)
            t = lax.dot_general(own[:, at], q, NT, preferred_element_type=jnp.float32)
            t = jnp.where(causal, t, NEG_FILL)
            top = jnp.maximum(
                jnp.max(s, axis=0, keepdims=True), jnp.max(t, axis=0, keepdims=True)
            )
            total = jnp.sum(jnp.exp2((s - top) * EXP2_SCALE), axis=0, keepdims=True)
            total += jnp.sum(jnp.exp2((t - top) * EXP2_SCALE), axis=0, keepdims=True)
            lse[me, b, head : head + 1, :] = top * SCALE + jnp.log(total)

    lse[me] = jnp.zeros(lse.shape[1:], jnp.float32)
    each_block(stats)
    for offset in reversed(range(1, n)):
        send_lse(offset, me).start()

    def keep_scores(b):
        if blocks > 1:
            gather_block(b)
        for head in range(kv_heads):
            at = slice(head * HEAD_SIZE, (head + 1) * HEAD_SIZE)
            scores[b, head] = lax.dot_general(
                queries_of(head), keys[:, at], NT, preferred_element_type=jnp.float32
            )

    each_block(keep_scores)
    for offset in range(1, n):
        send_lse(offset, peer(offset)).wait_recv()

    for offset in range(1, n):
        send_q(offset, me).wait_send()
        send_lse(offset, me).wait_send()


def finish_kernel(scores, lse, out_ref):
    blocks, kv_heads, used, _ = scores.shape
    out_ref[...] = jnp.full(out_ref.shape, -jnp.inf, jnp.float32)

    def finish(b):
        parts = lse[:, b]
        top = jnp.max(parts, axis=0)
        shift = top + jnp.log(jnp.sum(jnp.exp(parts - top[None]), axis=0))
        columns = jnp.transpose(shift)
        for head in range(kv_heads):
            best = jnp.max(
                scores[b, head] * SCALE - columns[:used, head : head + 1], axis=0, keepdims=True
            )
            out_ref[head : head + 1, :] = jnp.maximum(out_ref[head : head + 1, :], best)

    if blocks == 1:
        finish(0)
    else:
        lax.fori_loop(0, blocks, lambda b, c: (finish(b), c)[1], 0)


def solution(mesh):
    n = mesh.shape["ctx"]

    def on_device(queries, repeat_block_keys, context_keys):
        per, width = queries.shape
        cache_len, key_width = context_keys.shape
        kv_heads = key_width // HEAD_SIZE
        group = width // key_width
        blocks = n * per // BLOCK_ROWS
        assert blocks * BLOCK_ROWS == n * per
        held_bytes = 4 * blocks * kv_heads * group * BLOCK_ROWS * cache_len
        resident = held_bytes <= RESIDENT_BYTES
        held = pltpu.VMEM if resident else jax.ShapeDtypeStruct
        finish_limit = RESIDENT_LIMIT if resident else None
        scores, lse = pl.pallas_call(
            functools.partial(kernel, n, group),
            out_shape=[
                held((blocks, kv_heads, group * BLOCK_ROWS, cache_len), jnp.float32),
                held((n, blocks, 8, LANES), jnp.float32),
            ],
            in_specs=[pl.BlockSpec(memory_space=pl.ANY)] * 3,
            out_specs=[pl.BlockSpec(memory_space=pltpu.VMEM)] * 2,
            scratch_shapes=[
                pltpu.VMEM((n, per, width), jnp.bfloat16),
                pltpu.VMEM((per, key_width), jnp.bfloat16),
                pltpu.VMEM((cache_len, key_width), jnp.bfloat16),
                pltpu.VMEM((BLOCK_ROWS, width), jnp.float32),
                pltpu.SemaphoreType.DMA((n,)),
                pltpu.SemaphoreType.DMA((n,)),
                pltpu.SemaphoreType.DMA((n,)),
                pltpu.SemaphoreType.DMA((n,)),
                pltpu.SemaphoreType.DMA((3,)),
            ],
            compiler_params=pltpu.CompilerParams(collective_id=0, has_side_effects=True),
        )(queries, repeat_block_keys, context_keys)
        return pl.pallas_call(
            finish_kernel,
            out_shape=jax.ShapeDtypeStruct((kv_heads, cache_len), jnp.float32),
            in_specs=[pl.BlockSpec(memory_space=pltpu.VMEM)] * 2,
            out_specs=pl.BlockSpec(memory_space=pltpu.VMEM),
            compiler_params=pltpu.CompilerParams(vmem_limit_bytes=finish_limit),
        )(scores, lse)

    placed = (P(("req", "ctx"), "tp"), P(("req", "ctx"), "tp"), P(("req", "ctx"), "tp"))
    return jax.shard_map(
        on_device, mesh=mesh, in_specs=placed, out_specs=P("tp", ("req", "ctx")), check_vma=False
    )
```

```python
import functools
import math

import jax
import jax.numpy as jnp
from jax import lax
from jax.experimental import pallas as pl
from jax.experimental.pallas import tpu as pltpu
from jax.sharding import PartitionSpec as P

HEAD_SIZE = 128
LANES = 128
BLOCK_ROWS = 16
NEG_FILL = -1e30
RESIDENT_BYTES = 2 << 20
RESIDENT_LIMIT = 8 << 20
SCALE = 1.0 / math.sqrt(HEAD_SIZE)
EXP2_SCALE = SCALE * math.log2(math.e)
NT = (((1,), (1,)), ((), ()))


def kernel(
    n, group, q_ref, own_ref, k_ref, scores, lse,
    q_all, own, keys, q_block,
    q_send, q_recv, l_send, l_recv, local_sem,
):
    me = lax.axis_index("ctx")
    per = q_ref.shape[0]
    kv_heads = k_ref.shape[1] // HEAD_SIZE
    peers_per_block = BLOCK_ROWS // per
    blocks = n // peers_per_block
    used = group * BLOCK_ROWS
    turn = 1 - 2 * (me // (n // 2))
    peer = lambda offset: lax.rem(me + turn * offset + n, n)

    load_keys = pltpu.make_async_copy(k_ref, keys, local_sem.at[0])
    load_own = pltpu.make_async_copy(own_ref, own, local_sem.at[1])
    load_q = pltpu.make_async_copy(q_ref, q_all.at[me], local_sem.at[2])

    barrier = pltpu.get_barrier_semaphore()
    for offset in reversed(range(1, n)):
        pl.semaphore_signal(
            barrier, inc=1, device_id={"ctx": peer(offset)}, device_id_type=pl.DeviceIdType.MESH
        )
    load_q.start()
    load_own.start()
    load_keys.start()
    load_q.wait()
    pl.semaphore_wait(barrier, n - 1)

    def send_q(offset, slot):
        return pltpu.make_async_remote_copy(
            src_ref=q_all.at[me],
            dst_ref=q_all.at[slot],
            send_sem=q_send,
            recv_sem=q_recv,
            device_id={"ctx": peer(offset)},
            device_id_type=pl.DeviceIdType.MESH,
        )

    def everyone(slots, send, recv):
        return pltpu.make_async_remote_copy(
            src_ref=slots.at[pl.ds(0, n - 1)],
            dst_ref=slots.at[pl.ds(0, n - 1)],
            send_sem=send,
            recv_sem=recv,
            device_id={"ctx": peer(1)},
            device_id_type=pl.DeviceIdType.MESH,
        )

    def send_lse(offset, slot):
        return pltpu.make_async_remote_copy(
            src_ref=lse.at[slot],
            dst_ref=lse.at[slot],
            send_sem=l_send,
            recv_sem=l_recv,
            device_id={"ctx": peer(offset)},
            device_id_type=pl.DeviceIdType.MESH,
        )

    for offset in reversed(range(1, n)):
        send_q(offset, me).start()
    load_own.wait()
    load_keys.wait()
    everyone(q_all, q_send, q_recv).wait_recv()

    def each_block(body):
        if blocks == 1:
            body(0)
        else:
            lax.fori_loop(0, blocks, lambda b, c: (body(b), c)[1], 0)

    def queries_of(head):
        return jnp.concatenate(
            [
                q_block[:, (head * group + u) * HEAD_SIZE : (head * group + u + 1) * HEAD_SIZE]
                for u in range(group)
            ],
            axis=0,
        ).astype(jnp.bfloat16)

    def gather_block(b):
        for p in range(peers_per_block):
            q_block[p * per : (p + 1) * per, :] = q_all[b * peers_per_block + p].astype(jnp.float32)

    def stats(b):
        gather_block(b)
        lane = lax.broadcasted_iota(jnp.int32, (per, LANES), 1)
        row = b * BLOCK_ROWS + lax.rem(lane, BLOCK_ROWS)
        column = me * per + lax.broadcasted_iota(jnp.int32, (per, LANES), 0)
        causal = column <= row
        pad = jnp.zeros((LANES - used, HEAD_SIZE), jnp.bfloat16)
        for head in range(kv_heads):
            at = slice(head * HEAD_SIZE, (head + 1) * HEAD_SIZE)
            q = jnp.concatenate([queries_of(head), pad], axis=0)
            s = lax.dot_general(keys[:, at], q, NT, preferred_element_type=jnp.float32)
            t = lax.dot_general(own[:, at], q, NT, preferred_element_type=jnp.float32)
            t = jnp.where(causal, t, NEG_FILL)
            top = jnp.maximum(
                jnp.max(s, axis=0, keepdims=True), jnp.max(t, axis=0, keepdims=True)
            )
            total = jnp.sum(jnp.exp2((s - top) * EXP2_SCALE), axis=0, keepdims=True)
            total += jnp.sum(jnp.exp2((t - top) * EXP2_SCALE), axis=0, keepdims=True)
            lse[me, b, head : head + 1, :] = top * SCALE + jnp.log(total)

    lse[me] = jnp.zeros(lse.shape[1:], jnp.float32)
    each_block(stats)
    for offset in reversed(range(1, n)):
        send_lse(offset, me).start()

    def keep_scores(b):
        if blocks > 1:
            gather_block(b)
        for head in range(kv_heads):
            at = slice(head * HEAD_SIZE, (head + 1) * HEAD_SIZE)
            scores[b, head] = lax.dot_general(
                queries_of(head), keys[:, at], NT, preferred_element_type=jnp.float32
            )

    each_block(keep_scores)
    everyone(lse, l_send, l_recv).wait_recv()

    everyone(q_all, q_send, q_recv).wait_send()
    everyone(lse, l_send, l_recv).wait_send()


def finish_kernel(scores, lse, out_ref):
    blocks, kv_heads, used, _ = scores.shape
    out_ref[...] = jnp.full(out_ref.shape, -jnp.inf, jnp.float32)

    def finish(b):
        parts = lse[:, b]
        top = jnp.max(parts, axis=0)
        shift = top + jnp.log(jnp.sum(jnp.exp(parts - top[None]), axis=0))
        columns = jnp.transpose(shift)
        for head in range(kv_heads):
            best = jnp.max(
                scores[b, head] * SCALE - columns[:used, head : head + 1], axis=0, keepdims=True
            )
            out_ref[head : head + 1, :] = jnp.maximum(out_ref[head : head + 1, :], best)

    if blocks == 1:
        finish(0)
    else:
        lax.fori_loop(0, blocks, lambda b, c: (finish(b), c)[1], 0)


def solution(mesh):
    n = mesh.shape["ctx"]

    def on_device(queries, repeat_block_keys, context_keys):
        per, width = queries.shape
        cache_len, key_width = context_keys.shape
        kv_heads = key_width // HEAD_SIZE
        group = width // key_width
        blocks = n * per // BLOCK_ROWS
        assert blocks * BLOCK_ROWS == n * per
        held_bytes = 4 * blocks * kv_heads * group * BLOCK_ROWS * cache_len
        resident = held_bytes <= RESIDENT_BYTES
        held = pltpu.VMEM if resident else jax.ShapeDtypeStruct
        finish_limit = RESIDENT_LIMIT if resident else None
        scores, lse = pl.pallas_call(
            functools.partial(kernel, n, group),
            out_shape=[
                held((blocks, kv_heads, group * BLOCK_ROWS, cache_len), jnp.float32),
                held((n, blocks, 8, LANES), jnp.float32),
            ],
            in_specs=[pl.BlockSpec(memory_space=pl.ANY)] * 3,
            out_specs=[pl.BlockSpec(memory_space=pltpu.VMEM)] * 2,
            scratch_shapes=[
                pltpu.VMEM((n, per, width), jnp.bfloat16),
                pltpu.VMEM((per, key_width), jnp.bfloat16),
                pltpu.VMEM((cache_len, key_width), jnp.bfloat16),
                pltpu.VMEM((BLOCK_ROWS, width), jnp.float32),
                pltpu.SemaphoreType.DMA,
                pltpu.SemaphoreType.DMA,
                pltpu.SemaphoreType.DMA,
                pltpu.SemaphoreType.DMA,
                pltpu.SemaphoreType.DMA((3,)),
            ],
            compiler_params=pltpu.CompilerParams(collective_id=0, has_side_effects=True),
        )(queries, repeat_block_keys, context_keys)
        return pl.pallas_call(
            finish_kernel,
            out_shape=jax.ShapeDtypeStruct((kv_heads, cache_len), jnp.float32),
            in_specs=[pl.BlockSpec(memory_space=pltpu.VMEM)] * 2,
            out_specs=pl.BlockSpec(memory_space=pltpu.VMEM),
            compiler_params=pltpu.CompilerParams(vmem_limit_bytes=finish_limit),
        )(scores, lse)

    placed = (P(("req", "ctx"), "tp"), P(("req", "ctx"), "tp"), P(("req", "ctx"), "tp"))
    return jax.shard_map(
        on_device, mesh=mesh, in_specs=placed, out_specs=P("tp", ("req", "ctx")), check_vma=False
    )
```
